32 devices in a mesh: outer: 4 (over z), inner: 2 (over y), head: 4 (over x, core).
Axes of the slice: x: 2, y: 2, z: 4, core: 2. Of those that a mesh axis runs over, the one named last changes fastest.
Arguments:
- values: bfloat16 [8192, 4096], P(('outer', 'inner'), 'head'), may hold values from -40 to 40
- input_state: bfloat16 [8192, 128], P(('outer', 'inner')), may hold values from -0.5 to 0.5
- output_state: bfloat16 [8192, 128], P(('outer', 'inner')), may hold values from -6 to 6
- step_log_decay: float32 [64, 8192], P('head', ('outer', 'inner')), may hold values from -0.6 to 0
- level_gates: float32 [4, 64, 8192], P(None, 'head', ('outer', 'inner')), may hold values from 0.1 to 1
- norm_gain: float32 [4096], P('head'), may hold values from 0.25 to 1.75
Outputs:
- mixed: bfloat16 [8192, 4096], P(('outer', 'inner'), 'head')
The draws below stay inside these ranges and needn't reach their ends.
All inputs are finite; a program needn't handle non-finite values.
Results may differ from the reference program's by a relative error of at most 0.0051.
Values sent between devices are 32-bit elements; how exact they have to be, the bound alone decides.
A program may use at most 64 MiB of HBM per device.

```python
import math
import jax
import jax.numpy as jnp
from jax import lax

HEAD_TOTAL = 64
P_SIZE = 64
N = 128
TOK_DEV = 1024
SPAN = 256
SHARDS = 8
SEQUENCE_TOKENS = 8192
BITS = 3
LEVELS = 4
N_OUTER = 4
N_INNER = 2


def draw_values(key, part):
    key_sequence = jax.random.split(key, 3)
    row_scale = jnp.exp(jax.random.uniform(key_sequence[0], (SEQUENCE_TOKENS, 1), jnp.float32) * math.log(10.0))
    col_scale = jnp.exp(jax.random.uniform(key_sequence[1], (1, HEAD_TOTAL * P_SIZE), jnp.float32) * math.log(10.0))
    base_draw = jnp.clip(jax.random.normal(key_sequence[2], (SEQUENCE_TOKENS, HEAD_TOTAL * P_SIZE), jnp.float32), -4.0, 4.0)
    return (base_draw * row_scale * col_scale * 0.1).astype(jnp.bfloat16)


def draw_step_log_decay(key, part):
    key_sequence = jax.random.split(key, 9)
    fast_share = 0.5
    head_pick = jax.random.uniform(key_sequence[0], (HEAD_TOTAL, 1), jnp.float32)
    quick_heads = jnp.logical_or(head_pick < fast_share, head_pick <= jnp.min(head_pick))
    quick_rate = 1.0 / (30.0 + 20.0 * jax.random.uniform(key_sequence[1], (HEAD_TOTAL, 1), jnp.float32))
    slow_rate = jnp.exp(jax.random.uniform(key_sequence[2], (HEAD_TOTAL, 1), jnp.float32, math.log(0.1), math.log(0.6))) / SEQUENCE_TOKENS
    head_decay_rate = jnp.where(quick_heads, quick_rate, slow_rate)
    jitter_amount = jnp.exp(jax.random.uniform(key_sequence[3], (HEAD_TOTAL, SEQUENCE_TOKENS), jnp.float32, math.log(0.5), math.log(2.0)))
    brisk_block = jnp.exp(jax.random.uniform(key_sequence[4], (HEAD_TOTAL, SHARDS), jnp.float32, math.log(0.5), math.log(2.0)))
    drawn_block = jnp.exp(jax.random.uniform(key_sequence[7], (HEAD_TOTAL, SHARDS), jnp.float32, math.log(0.01), math.log(0.03)))
    parity = jax.random.randint(key_sequence[8], (HEAD_TOTAL, 1), 0, 2)
    drawn_mask = jnp.remainder(jnp.arange(SHARDS)[None, :] + parity, 2) == 0
    block_factor = jnp.where(drawn_mask, drawn_block, brisk_block)
    block_multiplier = jnp.repeat(block_factor, TOK_DEV, axis=1)
    spike_positions = jax.random.randint(key_sequence[5], (HEAD_TOTAL, 3, 1), 0, SEQUENCE_TOKENS)
    spike_mask = jnp.any(jnp.arange(SEQUENCE_TOKENS)[None, None, :] == spike_positions, axis=1)
    spike_penalty = jax.random.uniform(key_sequence[6], (HEAD_TOTAL, SEQUENCE_TOKENS), jnp.float32, 0.2, 0.35)
    return -head_decay_rate * jitter_amount * block_multiplier + jnp.where(spike_mask, jnp.log(1.0 - spike_penalty), 0.0)


def block_levels(own_key, dims, pieces, least, top_value):
    factor_of, own = 1.0, jax.random.fold_in(own_key, 6)
    for axis_at, shards_of in pieces:
        heights = jnp.exp(jax.random.uniform(jax.random.fold_in(own, axis_at), (shards_of,), jnp.float32, least / len(pieces), top_value / len(pieces)))
        factor_of = factor_of * jnp.repeat(heights, dims[axis_at] // shards_of).reshape([-1 if axis == axis_at else 1 for axis in range(len(dims))])
    return factor_of


def centred(rng, extent, scale, reach, pieces=(), kind=jnp.bfloat16):
    values = scale * jax.random.normal(rng, extent, jnp.float32)
    if pieces:
        values = values * block_levels(rng, extent, pieces, -0.22, 0.18)
    return jnp.clip(values, -reach, reach).astype(kind)


def setup_inputs(seed: int = 0) -> dict:
    keys = jax.random.split(jax.random.key(seed), 7)
    values = draw_values(jax.random.fold_in(keys[6], 71), 0)
    input_state = centred(keys[1], (SEQUENCE_TOKENS, N), 0.09, 0.5, ((0, 8),))
    output_state = centred(keys[2], (SEQUENCE_TOKENS, N), 1.0, 6.0, ((0, 8),))
    step_log_decay = draw_step_log_decay(jax.random.fold_in(keys[6], 71), 0)
    level_gates = jnp.clip(jnp.exp(math.log(1.0) - 2.3025851 * jax.random.uniform(keys[4], (LEVELS, HEAD_TOTAL, SEQUENCE_TOKENS), jnp.float32) ** block_levels(keys[4], (LEVELS, HEAD_TOTAL, SEQUENCE_TOKENS), ((1, 4), (2, 8)), -0.2, 0.2)), 0.1, 1.0)
    norm_gain = jnp.clip(1.0 + 0.15 * jax.random.normal(keys[5], (HEAD_TOTAL * P_SIZE,), jnp.float32), 0.25, 1.75)
    return {"values": values, "input_state": input_state, "output_state": output_state, "step_log_decay": step_log_decay, "level_gates": level_gates, "norm_gain": norm_gain}


def to_half(array):
    return lax.optimization_barrier(array.astype(jnp.bfloat16)).astype(jnp.float32)

def piece_scan(values_split, in_rows, out_rows, log_decay, with_local):
    tokens = values_split.shape[0]
    head_count = values_split.shape[1]
    piece_count = tokens // SPAN
    val_pieces = values_split.reshape(piece_count, SPAN, head_count, P_SIZE).astype(jnp.float32)
    in_pieces = in_rows.reshape(piece_count, SPAN, N)
    out_pieces = out_rows.reshape(piece_count, SPAN, N)
    decay_pieces = log_decay.reshape(head_count, piece_count, SPAN).transpose(1, 0, 2)
    causal = jnp.arange(SPAN)[:, None] >= jnp.arange(SPAN)[None, :]

    def advance(scan_carry, inputs):
        block_state, offset = scan_carry
        val_piece, in_piece, out_piece, decay_piece = inputs
        running = jnp.cumsum(decay_piece, axis=1)
        piece_total = running[:, -1]
        weighted = to_half(in_piece.astype(jnp.float32)[None] * jnp.exp(piece_total[:, None] - running)[:, :, None])
        fresh_state = jnp.einsum('shp,hsn->hpn', val_piece, weighted)
        if with_local:
            scores = jnp.dot(out_piece, in_piece.T, preferred_element_type=jnp.float32)
            spread = running[:, :, None] - running[:, None, :]
            fading = jnp.exp(jnp.where(causal[None], spread, -jnp.inf))
            mixing = to_half(scores[None] * fading)
            within = jnp.einsum('hts,shp->thp', mixing, val_piece)
            earlier = jnp.einsum('tn,hpn->thp', out_piece.astype(jnp.float32), to_half(block_state))
            level_zero = within + earlier * jnp.exp(running).T[:, :, None]
        else:
            level_zero = jnp.zeros((SPAN, head_count, P_SIZE), jnp.float32)
        block_state = jnp.exp(piece_total)[:, None, None] * block_state + fresh_state
        return ((block_state, offset + piece_total), (level_zero, running + offset[:, None]))
    start = (jnp.zeros((head_count, P_SIZE, N), jnp.float32), jnp.zeros((head_count,), jnp.float32))
    final, outputs = lax.scan(advance, start, (val_pieces, in_pieces, out_pieces, decay_pieces))
    level_zero = outputs[0].reshape(tokens, head_count, P_SIZE)
    cum = outputs[1].transpose(1, 0, 2).reshape(head_count, tokens)
    return (final[0], final[1], level_zero, cum)

def far_terms(out_rows, buckets, gap_list, upper_flags, upper_gates, cum):
    stacked = jnp.stack(buckets)
    level_count, head_count, head_width, state_size = stacked.shape
    tokens = out_rows.shape[0]
    products = jnp.einsum('tn,lkn->ltk', out_rows.astype(jnp.float32), stacked.reshape(level_count, head_count * head_width, state_size), precision=lax.Precision.HIGHEST)
    weights = upper_gates * jnp.stack(upper_flags)[:, None, None] * jnp.exp(cum[None] + jnp.stack(gap_list)[:, :, None])
    return lax.optimization_barrier(jnp.sum(products.reshape(level_count, tokens, head_count, head_width) * jnp.transpose(weights, (0, 2, 1))[:, :, :, None], axis=0))

def reference(values, input_state, output_state, step_log_decay, level_gates, norm_gain):
    shard_count = N_OUTER * N_INNER
    value_blocks = values.reshape(shard_count, TOK_DEV, HEAD_TOTAL, P_SIZE)
    in_blocks = input_state.reshape(shard_count, TOK_DEV, N)
    out_blocks = output_state.reshape(shard_count, TOK_DEV, N)
    decay_blocks = step_log_decay.reshape(HEAD_TOTAL, shard_count, TOK_DEV).transpose(1, 0, 2)
    gate_blocks = level_gates.reshape(LEVELS, HEAD_TOTAL, shard_count, TOK_DEV).transpose(2, 0, 1, 3)

    def block_summary(block_item):
        summary = piece_scan(block_item[0], block_item[1], block_item[2], block_item[3], False)
        return (summary[0], summary[1])
    block_states, block_logs = lax.map(block_summary, (value_blocks, in_blocks, out_blocks, decay_blocks))
    tree_states = [block_states]
    tree_logs = [block_logs]
    for step_bit in range(BITS):
        lower_states = tree_states[-1]
        lower_logs = tree_logs[-1]
        tree_states.append(jnp.exp(lower_logs[1::2])[:, :, None, None] * lower_states[0::2] + lower_states[1::2])
        tree_logs.append(lower_logs[0::2] + lower_logs[1::2])
    gain_grid = norm_gain.reshape(HEAD_TOTAL, P_SIZE)

    def block_output(block_item):
        position, value_block, in_block, out_block, decay_block, gate_block = block_item
        summary = piece_scan(value_block, in_block, out_block, decay_block, True)
        level_zero = summary[2]
        cum = summary[3]
        buckets = []
        gap_list = []
        upper_flags = []
        running_gap = jnp.zeros((HEAD_TOTAL,), jnp.float32)
        for step_bit in range(BITS):
            mine_group = jnp.right_shift(position, step_bit)
            sibling = jnp.bitwise_xor(mine_group, 1).astype(jnp.int32)
            upper_flag = jnp.bitwise_and(mine_group, 1).astype(jnp.float32)
            buckets.append(lax.dynamic_index_in_dim(tree_states[step_bit], sibling, 0, keepdims=False))
            gap_list.append(running_gap)
            upper_flags.append(upper_flag)
            running_gap = running_gap + upper_flag * lax.dynamic_index_in_dim(tree_logs[step_bit], sibling, 0, keepdims=False)
        combined = gate_block[0].T[:, :, None] * level_zero + far_terms(out_block, buckets, gap_list, upper_flags, gate_block[1:], cum)
        mean_square = lax.optimization_barrier(jnp.mean(combined * combined, axis=2, keepdims=True))
        return (combined * lax.rsqrt(mean_square + 1e-05) * gain_grid).astype(jnp.bfloat16).reshape(TOK_DEV, HEAD_TOTAL * P_SIZE)
    positions = jnp.arange(shard_count, dtype=jnp.int32)
    mixed = lax.map(block_output, (positions, value_blocks, in_blocks, out_blocks, decay_blocks, gate_blocks))
    return mixed.reshape(shard_count * TOK_DEV, HEAD_TOTAL * P_SIZE)
```

```python
import functools

import jax
import jax.numpy as jnp
from jax import lax
from jax.experimental import pallas as pl
from jax.experimental.pallas import tpu as pltpu
from jax.sharding import PartitionSpec as P

P_SIZE = 64
N = 128
STEP = 128
LANES = 256
FAR_ROWS = 256
F32 = jnp.float32
BF16 = jnp.bfloat16
MESH = pl.DeviceIdType.MESH
EXACT = lax.Precision.HIGHEST


def dot(a, b, precision=None):
    return jnp.dot(a, b, preferred_element_type=F32, precision=precision)


def split_two(x):
    high = x.astype(BF16)
    return high, (x - high.astype(F32)).astype(BF16)


def kernel(
    n_outer,
    n_inner,
    v_ref,
    b_ref,
    c_ref,
    d_ref,
    g_ref,
    gain_ref,
    o_ref,
    w_ref,
    e_ref,
    bt_ref,
    x_ref,
    r_ref,
    rows_ref,
    gap_ref,
    acc_ref,
    agg_ref,
    got_ref,
    send_sem,
    pass_sem,
    recv_sem,
):
    tokens, width = v_ref.shape
    heads = d_ref.shape[0]
    steps = tokens // STEP
    chunks = width // LANES
    inner_bits = n_inner.bit_length() - 1
    outer_bits = n_outer.bit_length() - 1
    bits = inner_bits + outer_bits
    outer = lax.axis_index("outer")
    inner = lax.axis_index("inner")

    def bit_of(number, bit):
        return lax.rem(number // (1 << bit), 2)

    def flipped(bit):
        return inner + (1 - 2 * bit_of(inner, bit)) * (1 << bit)

    barrier = pltpu.get_barrier_semaphore()
    for bit in range(inner_bits):
        pl.semaphore_signal(barrier, inc=1, device_id={"inner": flipped(bit)}, device_id_type=MESH)

    @pl.when(outer > 0)
    def _():
        pl.semaphore_signal(barrier, inc=1, device_id={"outer": outer - 1}, device_id_type=MESH)

    @pl.when(outer < n_outer - 1)
    def _():
        pl.semaphore_signal(barrier, inc=1, device_id={"outer": outer + 1}, device_id_type=MESH)

    row_i = lax.broadcasted_iota(jnp.int32, (STEP, STEP), 0)
    col_i = lax.broadcasted_iota(jnp.int32, (STEP, STEP), 1)
    upto = (row_i <= col_i).astype(F32)
    spread_f = (
        lax.broadcasted_iota(jnp.int32, (heads, width), 1) // P_SIZE
        == lax.broadcasted_iota(jnp.int32, (heads, width), 0)
    ).astype(F32)
    e_ref[...] = jnp.concatenate([spread_f, spread_f], axis=0).astype(BF16)
    stacked = jnp.concatenate(
        [d_ref[:, c * STEP : (c + 1) * STEP] for c in range(steps)], axis=0
    )
    run_all = dot(stacked, upto, EXACT)
    offset = jnp.zeros((heads, 1), F32)
    last_columns = []
    for c in range(steps):
        span = slice(c * STEP, (c + 1) * STEP)
        run = run_all[c * heads : (c + 1) * heads]
        last = run[:, STEP - 1 : STEP]
        last_columns.append(last)
        centre = 0.5 * last
        grown = jnp.exp(run - centre)
        cum_exp = jnp.exp(run + offset)
        kinds = [jnp.exp(centre - run), g_ref[0, :, span] * grown]
        for bit in range(bits):
            kinds.append(g_ref[bit + 1, :, span] * cum_exp)
        for kind, weight in enumerate(kinds):
            high = weight.astype(BF16).astype(F32)
            both = jnp.concatenate([high, weight - high], axis=0)
            w_ref[kind, span, :] = both.T.astype(BF16)
        offset = offset + last
        bt_ref[c] = b_ref[span, :].astype(F32).T.astype(BF16)
        scores = lax.dot_general(
            c_ref[span, :],
            b_ref[span, :],
            (((1,), (1,)), ((), ())),
            preferred_element_type=F32,
        )
        x_ref[span, 0:STEP] = jnp.where(row_i >= col_i, scores, 0.0).astype(BF16)
        x_ref[span, STEP:] = c_ref[span, :]
    step_logs = jnp.concatenate(
        [jnp.broadcast_to(last, (heads, STEP)) for last in last_columns], axis=0
    )
    for c in range(steps):
        one = step_logs[c * heads : (c + 1) * heads].T[0:8]
        rows_ref[c] = dot(one, spread_f, EXACT)

    def lanes(q):
        return slice(q * LANES, (q + 1) * LANES)

    def weight_of(kind, rows, q):
        return dot(w_ref[kind, rows, :], e_ref[:, lanes(q)])

    def copy_to(source, level, q, sem, device):
        return pltpu.make_async_remote_copy(
            src_ref=source,
            dst_ref=got_ref.at[level, q],
            send_sem=sem.at[level, q],
            recv_sem=recv_sem.at[level, q],
            device_id=device,
            device_id_type=MESH,
        )

    def halved(level):
        return inner_bits > 0 and level > inner_bits

    def mine(q):
        return lax.rem(inner, 2) == q % 2

    def outer_sends(level, q, action):
        bit = level - inner_bits
        goes = jnp.logical_and(outer < n_outer - 1, bit_of(outer + 1, bit) == 1)
        if halved(level):
            goes = jnp.logical_and(goes, mine(q))
        return goes, bit

    def start_outer(level, q, from_agg):
        goes, bit = outer_sends(level, q, None)
        kind = bit_of(outer, bit) == (0 if from_agg else 1)
        source = agg_ref.at[level, q] if from_agg else got_ref.at[level, q]

        @pl.when(jnp.logical_and(goes, kind))
        def _():
            copy_to(source, level, q, send_sem, {"outer": outer + 1}).start()

    def start_level(level, q):
        if level >= bits:
            return
        if level < inner_bits:
            copy_to(
                agg_ref.at[level, q], level, q, send_sem, {"inner": flipped(level)}
            ).start()
        else:
            start_outer(level, q, True)

    def near(q):
        state = jnp.zeros((N, LANES), F32)
        total = jnp.zeros((8, LANES), F32)
        for c in range(steps):
            span = slice(c * STEP, (c + 1) * STEP)
            scaled = (v_ref[span, lanes(q)].astype(F32) * weight_of(0, span, q)).astype(BF16)
            log_rows = rows_ref[c, :, lanes(q)]
            factor = jnp.exp(0.5 * log_rows[0:1])
            shrunk = factor * state
            r_ref[c, 0:STEP, lanes(q)] = scaled
            r_ref[c, STEP:, lanes(q)] = shrunk.astype(BF16)
            state = factor * (shrunk + dot(bt_ref[c], scaled))
            total = total + log_rows
        agg_ref[0, q, 0:N] = state
        agg_ref[0, q, N:] = total
        gap_ref[q] = jnp.zeros((8, LANES), F32)

    def local(q):
        for c in range(steps):
            span = slice(c * STEP, (c + 1) * STEP)
            acc_ref[span, lanes(q)] = dot(x_ref[span, :], r_ref[c, :, lanes(q)]) * weight_of(
                1, span, q
            )

    def far(level, q):
        gap = gap_ref[q]
        bucket = got_ref[level, q, 0:N] * jnp.exp(gap[0:1])
        gap_ref[q] = gap + got_ref[level, q, N:]
        high, low = split_two(bucket)
        right = jnp.concatenate([high, low], axis=0)
        for t in range(tokens // FAR_ROWS):
            span = slice(t * FAR_ROWS, (t + 1) * FAR_ROWS)
            left = x_ref[span, STEP:]
            product = dot(jnp.concatenate([left, left], axis=1), right)
            acc_ref[span, lanes(q)] += product * weight_of(2 + level, span, q)

    def merge(level, q, lower, upper):
        upper_log = upper[N:]
        agg_ref[level + 1, q, 0:N] = jnp.exp(upper_log[0:1]) * lower[0:N] + upper[0:N]
        agg_ref[level + 1, q, N:] = lower[N:] + upper_log

    def wait_got(level, q):
        copy_to(got_ref.at[level, q], level, q, send_sem, {"inner": inner}).wait_recv()

    def handle(level, q):
        if level < inner_bits:
            wait_got(level, q)
            upper = bit_of(inner, level) == 1
            if level + 1 < bits:

                @pl.when(upper)
                def _():
                    merge(level, q, got_ref.at[level, q], agg_ref.at[level, q])

                @pl.when(jnp.logical_not(upper))
                def _():
                    merge(level, q, agg_ref.at[level, q], got_ref.at[level, q])

                start_level(level + 1, q)
            pl.when(upper)(lambda: far(level, q))
            return
        bit = level - inner_bits

        @pl.when(bit_of(outer, bit) == 1)
        def _():
            wait_got(level, q)
            start_outer(level, q, False)
            if halved(level):

                @pl.when(mine(q))
                def _():
                    copy_to(
                        got_ref.at[level, q], level, q, pass_sem, {"inner": flipped(0)}
                    ).start()

            if level + 1 < bits:
                merge(level, q, got_ref.at[level, q], agg_ref.at[level, q])
                start_level(level + 1, q)
            far(level, q)

    averaging = (
        lax.broadcasted_iota(jnp.int32, (LANES, LANES), 0) // P_SIZE
        == lax.broadcasted_iota(jnp.int32, (LANES, LANES), 1) // P_SIZE
    )
    averaging = jnp.where(averaging, 1.0 / P_SIZE, 0.0).astype(BF16)

    def finish(q):
        gain = gain_ref[:, lanes(q)]
        for t in range(tokens // FAR_ROWS):
            span = slice(t * FAR_ROWS, (t + 1) * FAR_ROWS)
            combined = acc_ref[span, lanes(q)]
            mean_square = dot((combined * combined).astype(BF16), averaging)
            o_ref[span, lanes(q)] = (
                combined * lax.rsqrt(mean_square + 1e-05) * gain
            ).astype(BF16)

    for q in range(chunks):
        near(q)
        if q == 0:
            below = (outer + n_outer - 1) // n_outer
            above = 1 - (outer + 1) // n_outer
            pl.semaphore_wait(barrier, inner_bits + below + above)
        start_level(0, q)
    for tick in range(chunks + bits - 1):
        if tick < chunks:
            local(tick)
        for level in range(bits):
            q = tick - level
            if 0 <= q < chunks:
                handle(level, q)
                if level == bits - 1:
                    finish(q)
    for level in range(bits):
        for q in range(chunks):
            if level < inner_bits:
                copy_to(
                    agg_ref.at[level, q], level, q, send_sem, {"inner": flipped(level)}
                ).wait_send()
                continue
            goes, bit = outer_sends(level, q, None)

            @pl.when(goes)
            def _():
                copy_to(
                    agg_ref.at[level, q], level, q, send_sem, {"inner": inner}
                ).wait_send()

            if halved(level):

                @pl.when(jnp.logical_and(bit_of(outer, bit) == 1, mine(q)))
                def _():
                    copy_to(
                        got_ref.at[level, q], level, q, pass_sem, {"inner": flipped(0)}
                    ).wait_send()


def per_device(n_outer, n_inner, values, input_state, output_state, decay, gates, gain):
    tokens, width = values.shape
    heads = decay.shape[0]
    bits = n_outer.bit_length() + n_inner.bit_length() - 2
    steps, chunks = tokens // STEP, width // LANES
    flight = (bits, chunks, N + 8, LANES)
    in_vmem = pl.BlockSpec(memory_space=pltpu.VMEM)
    return pl.pallas_call(
        functools.partial(kernel, n_outer, n_inner),
        out_shape=jax.ShapeDtypeStruct((tokens, width), BF16),
        in_specs=[in_vmem] * 6,
        out_specs=in_vmem,
        scratch_shapes=[
            pltpu.VMEM((2 + bits, tokens, 2 * heads), BF16),
            pltpu.VMEM((2 * heads, width), BF16),
            pltpu.VMEM((steps, N, STEP), BF16),
            pltpu.VMEM((tokens, STEP + N), BF16),
            pltpu.VMEM((steps, STEP + N, width), BF16),
            pltpu.VMEM((steps, 8, width), F32),
            pltpu.VMEM((chunks, 8, LANES), F32),
            pltpu.VMEM((tokens, width), F32),
            pltpu.VMEM(flight, F32),
            pltpu.VMEM(flight, F32),
            pltpu.SemaphoreType.DMA((bits, chunks)),
            pltpu.SemaphoreType.DMA((bits, chunks)),
            pltpu.SemaphoreType.DMA((bits, chunks)),
        ],
        compiler_params=pltpu.CompilerParams(
            collective_id=0, has_side_effects=True, vmem_limit_bytes=56 * 1024 * 1024
        ),
    )(values, input_state, output_state, decay, gates, gain.reshape(1, width))


def solution(mesh):
    sequence = ("outer", "inner")
    return jax.shard_map(
        functools.partial(per_device, mesh.shape["outer"], mesh.shape["inner"]),
        mesh=mesh,
        in_specs=(
            P(sequence, "head"),
            P(sequence, None),
            P(sequence, None),
            P("head", sequence),
            P(None, "head", sequence),
            P("head"),
        ),
        out_specs=P(sequence, "head"),
        check_vma=False,
    )
```

```python
import functools

import jax
import jax.numpy as jnp
from jax import lax
from jax.experimental import pallas as pl
from jax.experimental.pallas import tpu as pltpu
from jax.sharding import PartitionSpec as P

P_SIZE = 64
N = 128
STEP = 128
LANES = 256
UNIT = 128
FAR_ROWS = 256
F32 = jnp.float32
BF16 = jnp.bfloat16
MESH = pl.DeviceIdType.MESH
EXACT = lax.Precision.HIGHEST


def dot(a, b, precision=None):
    return jnp.dot(a, b, preferred_element_type=F32, precision=precision)


def split_two(x):
    high = x.astype(BF16)
    return high, (x - high.astype(F32)).astype(BF16)


def kernel(
    n_outer,
    n_inner,
    v_ref,
    b_ref,
    c_ref,
    d_ref,
    g_ref,
    gain_ref,
    o_ref,
    w_ref,
    e_ref,
    bt_ref,
    x_ref,
    r_ref,
    rows_ref,
    gap_ref,
    acc_ref,
    agg_ref,
    got_ref,
    send_sem,
    pass_sem,
    recv_sem,
):
    tokens, width = v_ref.shape
    heads = d_ref.shape[0]
    steps = tokens // STEP
    chunks = width // LANES
    inner_bits = n_inner.bit_length() - 1
    outer_bits = n_outer.bit_length() - 1
    bits = inner_bits + outer_bits
    outer = lax.axis_index("outer")
    inner = lax.axis_index("inner")

    def bit_of(number, bit):
        return lax.rem(number // (1 << bit), 2)

    def flipped(bit):
        return inner + (1 - 2 * bit_of(inner, bit)) * (1 << bit)

    barrier = pltpu.get_barrier_semaphore()
    for bit in range(inner_bits):
        pl.semaphore_signal(barrier, inc=1, device_id={"inner": flipped(bit)}, device_id_type=MESH)

    @pl.when(outer > 0)
    def _():
        pl.semaphore_signal(barrier, inc=1, device_id={"outer": outer - 1}, device_id_type=MESH)

    @pl.when(outer < n_outer - 1)
    def _():
        pl.semaphore_signal(barrier, inc=1, device_id={"outer": outer + 1}, device_id_type=MESH)

    row_i = lax.broadcasted_iota(jnp.int32, (STEP, STEP), 0)
    col_i = lax.broadcasted_iota(jnp.int32, (STEP, STEP), 1)
    upto = (row_i <= col_i).astype(F32)
    spread_f = (
        lax.broadcasted_iota(jnp.int32, (heads, width), 1) // P_SIZE
        == lax.broadcasted_iota(jnp.int32, (heads, width), 0)
    ).astype(F32)
    e_ref[...] = jnp.concatenate([spread_f, spread_f], axis=0).astype(BF16)
    stacked = jnp.concatenate(
        [d_ref[:, c * STEP : (c + 1) * STEP] for c in range(steps)], axis=0
    )
    run_all = dot(stacked, upto, EXACT)
    offset = jnp.zeros((heads, 1), F32)
    last_columns = []
    for c in range(steps):
        span = slice(c * STEP, (c + 1) * STEP)
        run = run_all[c * heads : (c + 1) * heads]
        last = run[:, STEP - 1 : STEP]
        last_columns.append(last)
        centre = 0.5 * last
        grown = jnp.exp(run - centre)
        cum_exp = jnp.exp(run + offset)
        kinds = [jnp.exp(centre - run), g_ref[0, :, span] * grown]
        for bit in range(bits):
            kinds.append(g_ref[bit + 1, :, span] * cum_exp)
        for kind, weight in enumerate(kinds):
            high = weight.astype(BF16).astype(F32)
            both = jnp.concatenate([high, weight - high], axis=0)
            w_ref[kind, span, :] = both.T.astype(BF16)
        offset = offset + last
        bt_ref[c] = b_ref[span, :].astype(F32).T.astype(BF16)
        scores = lax.dot_general(
            c_ref[span, :],
            b_ref[span, :],
            (((1,), (1,)), ((), ())),
            preferred_element_type=F32,
        )
        x_ref[span, 0:STEP] = jnp.where(row_i >= col_i, scores, 0.0).astype(BF16)
        x_ref[span, STEP:] = c_ref[span, :]
    step_logs = jnp.concatenate(
        [jnp.broadcast_to(last, (heads, STEP)) for last in last_columns], axis=0
    )
    for c in range(steps):
        one = step_logs[c * heads : (c + 1) * heads].T[0:8]
        rows_ref[c] = dot(one, spread_f, EXACT)

    def lanes(q):
        return slice(q * LANES, (q + 1) * LANES)

    def weight_of(kind, rows, q):
        return dot(w_ref[kind, rows, :], e_ref[:, lanes(q)])

    parity = lax.rem(inner, 2)
    own_parity = (parity, 1 - parity)
    top_row = outer == n_outer - 1

    def unit_of(q, late):
        return 2 * q + own_parity[late]

    def copy_to(source, level, u, sem, device):
        return pltpu.make_async_remote_copy(
            src_ref=source,
            dst_ref=got_ref.at[level, u],
            send_sem=sem.at[level, u],
            recv_sem=recv_sem.at[level, u],
            device_id=device,
            device_id_type=MESH,
        )

    def halved(level):
        return inner_bits > 0 and level > inner_bits

    def skips(level, upper):
        return jnp.logical_and(top_row, upper) if level == inner_bits - 1 else None

    def unless(skip, action):
        if skip is None:
            action()
        else:
            pl.when(jnp.logical_not(skip))(action)

    def goes_up(level):
        bit = level - inner_bits
        return jnp.logical_and(outer < n_outer - 1, bit_of(outer + 1, bit) == 1)

    def own_up(level):
        return jnp.logical_and(goes_up(level), bit_of(outer, level - inner_bits) == 0)

    def pass_up(level):
        return jnp.logical_and(goes_up(level), bit_of(outer, level - inner_bits) == 1)

    def inner_copy(level, u):
        return copy_to(agg_ref.at[level, u], level, u, send_sem, {"inner": flipped(level)})

    def up_copy(source, level, u):
        return copy_to(source, level, u, send_sem, {"outer": outer + 1})

    def swap_copy(level, u):
        return copy_to(got_ref.at[level, u], level, u, pass_sem, {"inner": flipped(0)})

    def start_first(q, late):
        if inner_bits:
            u = unit_of(q, 1 - late)
            unless(skips(0, bit_of(inner, 0) == 1), lambda: inner_copy(0, u).start())
        else:
            u = unit_of(q, late)
            pl.when(own_up(0))(lambda: up_copy(agg_ref.at[0, u], 0, u).start())

    def merge(level, u, lower, upper):
        upper_log = upper[N:]
        agg_ref[level + 1, u, 0:N] = jnp.exp(upper_log[0:1]) * lower[0:N] + upper[0:N]
        agg_ref[level + 1, u, N:] = lower[N:] + upper_log

    def handle(level, q, late):
        u = unit_of(q, late)
        got, held = got_ref.at[level, u], agg_ref.at[level, u]
        if level < inner_bits:
            upper = bit_of(inner, level) == 1

            def take():
                inner_copy(level, u).wait_recv()
                following = level + 1
                if following == bits or (late and halved(following)):
                    return

                def join():
                    pl.when(upper)(lambda: merge(level, u, got, held))
                    pl.when(jnp.logical_not(upper))(lambda: merge(level, u, held, got))

                if following < inner_bits:
                    join()
                    unless(
                        skips(following, bit_of(inner, following) == 1),
                        lambda: inner_copy(following, u).start(),
                    )
                    return

                @pl.when(outer < n_outer - 1)
                def _():
                    join()

                @pl.when(own_up(following))
                def _():
                    up_copy(agg_ref.at[following, u], following, u).start()

            unless(skips(level, jnp.logical_not(upper)), take)
            return

        @pl.when(bit_of(outer, level - inner_bits) == 1)
        def _():
            up_copy(held, level, u).wait_recv()
            if late and halved(level):
                return

            @pl.when(pass_up(level))
            def _():
                up_copy(got, level, u).start()

            if halved(level):
                swap_copy(level, u).start()
            following = level + 1
            if following == bits or (late and halved(following)):
                return

            @pl.when(outer < n_outer - 1)
            def _():
                merge(level, u, got, held)

            @pl.when(own_up(following))
            def _():
                up_copy(agg_ref.at[following, u], following, u).start()

    def wait_sent(level, q, late):
        u = unit_of(q, late)
        if level < inner_bits:
            unless(
                skips(level, bit_of(inner, level) == 1),
                lambda: inner_copy(level, u).wait_send(),
            )
            return
        if late and halved(level):
            return
        pl.when(goes_up(level))(lambda: up_copy(agg_ref.at[level, u], level, u).wait_send())
        if halved(level):
            pl.when(bit_of(outer, level - inner_bits) == 1)(
                lambda: swap_copy(level, u).wait_send()
            )

    def needs(level):
        if level < inner_bits:
            return bit_of(inner, level) == 1
        return bit_of(outer, level - inner_bits) == 1

    def near(q):
        state = jnp.zeros((N, LANES), F32)
        total = jnp.zeros((8, LANES), F32)
        for c in range(steps):
            span = slice(c * STEP, (c + 1) * STEP)
            scaled = (v_ref[span, lanes(q)].astype(F32) * weight_of(0, span, q)).astype(BF16)
            log_rows = rows_ref[c, :, lanes(q)]
            factor = jnp.exp(0.5 * log_rows[0:1])
            shrunk = factor * state
            r_ref[c, 0:STEP, lanes(q)] = scaled
            r_ref[c, STEP:, lanes(q)] = shrunk.astype(BF16)
            state = factor * (shrunk + dot(bt_ref[c], scaled))
            total = total + log_rows
        for side in range(2):
            half = slice(side * UNIT, (side + 1) * UNIT)
            agg_ref[0, 2 * q + side, 0:N] = state[:, half]
            agg_ref[0, 2 * q + side, N:] = total[:, half]
        gap_ref[q] = jnp.zeros((8, LANES), F32)

    def local(q):
        for c in range(steps):
            span = slice(c * STEP, (c + 1) * STEP)
            acc_ref[span, lanes(q)] = dot(x_ref[span, :], r_ref[c, :, lanes(q)]) * weight_of(
                1, span, q
            )

    def far(level, q):
        gap = gap_ref[q]
        arrived = jnp.concatenate([got_ref[level, 2 * q], got_ref[level, 2 * q + 1]], axis=1)
        bucket = arrived[0:N] * jnp.exp(gap[0:1])
        gap_ref[q] = gap + arrived[N:]
        high, low = split_two(bucket)
        right = jnp.concatenate([high, low], axis=0)
        for t in range(tokens // FAR_ROWS):
            span = slice(t * FAR_ROWS, (t + 1) * FAR_ROWS)
            left = x_ref[span, STEP:]
            product = dot(jnp.concatenate([left, left], axis=1), right)
            acc_ref[span, lanes(q)] += product * weight_of(2 + level, span, q)

    averaging = (
        lax.broadcasted_iota(jnp.int32, (LANES, LANES), 0) // P_SIZE
        == lax.broadcasted_iota(jnp.int32, (LANES, LANES), 1) // P_SIZE
    )
    averaging = jnp.where(averaging, 1.0 / P_SIZE, 0.0).astype(BF16)

    def finish(q):
        gain = gain_ref[:, lanes(q)]
        for t in range(tokens // FAR_ROWS):
            span = slice(t * FAR_ROWS, (t + 1) * FAR_ROWS)
            combined = acc_ref[span, lanes(q)]
            mean_square = dot((combined * combined).astype(BF16), averaging)
            o_ref[span, lanes(q)] = (
                combined * lax.rsqrt(mean_square + 1e-05) * gain
            ).astype(BF16)

    for q in range(chunks):
        near(q)
        if q == 0:
            below = (outer + n_outer - 1) // n_outer
            above = 1 - (outer + 1) // n_outer
            pl.semaphore_wait(barrier, inner_bits + below + above)
        start_first(q, 0)
    for q in range(chunks):
        start_first(q, 1)
    events = []
    for level in range(bits):
        for late in range(2):
            for q in range(chunks):
                due = q + late * (chunks + 0.5) + 1.6 * level
                events.append((due, level, q, late))
    events.sort()
    for at, (_, level, q, late) in enumerate(events):
        handle(level, q, late)
        if at < chunks:
            local(at)
        if late:
            pl.when(needs(level))(lambda: far(level, q))
            if level == bits - 1:
                finish(q)
    for level in range(bits):
        for late in range(2):
            for q in range(chunks):
                wait_sent(level, q, late)


def per_device(n_outer, n_inner, values, input_state, output_state, decay, gates, gain):
    tokens, width = values.shape
    heads = decay.shape[0]
    bits = n_outer.bit_length() + n_inner.bit_length() - 2
    steps, chunks = tokens // STEP, width // LANES
    units = width // UNIT
    flight = (bits, units, N + 8, UNIT)
    in_vmem = pl.BlockSpec(memory_space=pltpu.VMEM)
    return pl.pallas_call(
        functools.partial(kernel, n_outer, n_inner),
        out_shape=jax.ShapeDtypeStruct((tokens, width), BF16),
        in_specs=[in_vmem] * 6,
        out_specs=in_vmem,
        scratch_shapes=[
            pltpu.VMEM((2 + bits, tokens, 2 * heads), BF16),
            pltpu.VMEM((2 * heads, width), BF16),
            pltpu.VMEM((steps, N, STEP), BF16),
            pltpu.VMEM((tokens, STEP + N), BF16),
            pltpu.VMEM((steps, STEP + N, width), BF16),
            pltpu.VMEM((steps, 8, width), F32),
            pltpu.VMEM((chunks, 8, LANES), F32),
            pltpu.VMEM((tokens, width), F32),
            pltpu.VMEM(flight, F32),
            pltpu.VMEM(flight, F32),
            pltpu.SemaphoreType.DMA((bits, units)),
            pltpu.SemaphoreType.DMA((bits, units)),
            pltpu.SemaphoreType.DMA((bits, units)),
        ],
        compiler_params=pltpu.CompilerParams(
            collective_id=0, has_side_effects=True, vmem_limit_bytes=56 * 1024 * 1024
        ),
    )(values, input_state, output_state, decay, gates, gain.reshape(1, width))


def solution(mesh):
    sequence = ("outer", "inner")
    return jax.shard_map(
        functools.partial(per_device, mesh.shape["outer"], mesh.shape["inner"]),
        mesh=mesh,
        in_specs=(
            P(sequence, "head"),
            P(sequence, None),
            P(sequence, None),
            P("head", sequence),
            P(None, "head", sequence),
            P("head"),
        ),
        out_specs=P(sequence, "head"),
        check_vma=False,
    )
```

```python
import functools

import jax
import jax.numpy as jnp
from jax import lax
from jax.experimental import pallas as pl
from jax.experimental.pallas import tpu as pltpu
from jax.sharding import PartitionSpec as P

P_SIZE = 64
N = 128
STEP = 128
LANES = 256
UNIT = 128
FAR_ROWS = 256
F32 = jnp.float32
BF16 = jnp.bfloat16
MESH = pl.DeviceIdType.MESH
EXACT = lax.Precision.HIGHEST


def dot(a, b, precision=None):
    return jnp.dot(a, b, preferred_element_type=F32, precision=precision)


def split_two(x):
    high = x.astype(BF16)
    return high, (x - high.astype(F32)).astype(BF16)


def kernel(
    n_outer,
    n_inner,
    v_hbm,
    b_hbm,
    c_hbm,
    d_hbm,
    g_hbm,
    gain_hbm,
    o_hbm,
    v_ref,
    b_ref,
    d_ref,
    gain_ref,
    c_ref,
    g_ref,
    o_ref,
    w_ref,
    e_ref,
    bt_ref,
    x_ref,
    r_ref,
    rows_ref,
    gap_ref,
    acc_ref,
    agg_ref,
    got_ref,
    send_sem,
    pass_sem,
    recv_sem,
    in_sem,
    out_sem,
):
    tokens, width = v_hbm.shape
    heads = d_hbm.shape[0]
    steps = tokens // STEP
    chunks = width // LANES
    inner_bits = n_inner.bit_length() - 1
    outer_bits = n_outer.bit_length() - 1
    bits = inner_bits + outer_bits
    outer = lax.axis_index("outer")
    inner = lax.axis_index("inner")
    v_copies = [
        pltpu.make_async_copy(v_hbm.at[:, span], v_ref.at[:, span], in_sem.at[q])
        for q, span in enumerate(
            pl.ds(first, LANES) for first in range(0, width, LANES)
        )
    ]
    g_copy = pltpu.make_async_copy(g_hbm, g_ref, in_sem.at[chunks])
    c_copy = pltpu.make_async_copy(c_hbm, c_ref, in_sem.at[chunks + 1])
    d_copy = pltpu.make_async_copy(d_hbm, d_ref, in_sem.at[chunks + 2])
    b_copy = pltpu.make_async_copy(b_hbm, b_ref, in_sem.at[chunks + 3])
    gain_copy = pltpu.make_async_copy(gain_hbm, gain_ref, in_sem.at[chunks + 4])
    for copy in [d_copy, b_copy] + v_copies + [g_copy, c_copy, gain_copy]:
        copy.start()

    def bit_of(number, bit):
        return lax.rem(number // (1 << bit), 2)

    def flipped(bit):
        return inner + (1 - 2 * bit_of(inner, bit)) * (1 << bit)

    barrier = pltpu.get_barrier_semaphore()
    for bit in range(inner_bits):
        pl.semaphore_signal(barrier, inc=1, device_id={"inner": flipped(bit)}, device_id_type=MESH)

    @pl.when(outer > 0)
    def _():
        pl.semaphore_signal(barrier, inc=1, device_id={"outer": outer - 1}, device_id_type=MESH)

    @pl.when(outer < n_outer - 1)
    def _():
        pl.semaphore_signal(barrier, inc=1, device_id={"outer": outer + 1}, device_id_type=MESH)

    row_i = lax.broadcasted_iota(jnp.int32, (STEP, STEP), 0)
    col_i = lax.broadcasted_iota(jnp.int32, (STEP, STEP), 1)
    upto = (row_i <= col_i).astype(F32)
    spread_f = (
        lax.broadcasted_iota(jnp.int32, (heads, width), 1) // P_SIZE
        == lax.broadcasted_iota(jnp.int32, (heads, width), 0)
    ).astype(F32)
    e_ref[...] = jnp.concatenate([spread_f, spread_f], axis=0).astype(BF16)
    d_copy.wait()
    b_copy.wait()
    stacked = jnp.concatenate(
        [d_ref[:, c * STEP : (c + 1) * STEP] for c in range(steps)], axis=0
    )
    run_all = dot(stacked, upto, EXACT)
    def put_weight(kind, span, weight):
        high = weight.astype(BF16).astype(F32)
        both = jnp.concatenate([high, weight - high], axis=0)
        w_ref[kind, span, :] = both.T.astype(BF16)

    def run_of(c):
        return run_all[c * heads : (c + 1) * heads]

    last_columns = []
    for c in range(steps):
        span = slice(c * STEP, (c + 1) * STEP)
        run = run_of(c)
        last = run[:, STEP - 1 : STEP]
        last_columns.append(last)
        put_weight(0, span, jnp.exp(0.5 * last - run))
        bt_ref[c] = b_ref[span, :].astype(F32).T.astype(BF16)

    def prepare_outputs():
        g_copy.wait()
        c_copy.wait()
        gain_copy.wait()
        offset = jnp.zeros((heads, 1), F32)
        for c in range(steps):
            span = slice(c * STEP, (c + 1) * STEP)
            run = run_of(c)
            put_weight(1, span, g_ref[0, :, span] * jnp.exp(run - 0.5 * last_columns[c]))
            cum_exp = jnp.exp(run + offset)
            for bit in range(bits):
                put_weight(2 + bit, span, g_ref[bit + 1, :, span] * cum_exp)
            offset = offset + last_columns[c]
            scores = lax.dot_general(
                c_ref[span, :],
                b_ref[span, :],
                (((1,), (1,)), ((), ())),
                preferred_element_type=F32,
            )
            x_ref[span, 0:STEP] = jnp.where(row_i >= col_i, scores, 0.0).astype(BF16)
            x_ref[span, STEP:] = c_ref[span, :]

    step_logs = jnp.concatenate(
        [jnp.broadcast_to(last, (heads, STEP)) for last in last_columns], axis=0
    )
    for c in range(steps):
        one = step_logs[c * heads : (c + 1) * heads].T[0:8]
        rows_ref[c] = dot(one, spread_f, EXACT)

    def lanes(q):
        return slice(q * LANES, (q + 1) * LANES)

    def weight_of(kind, rows, q):
        return dot(w_ref[kind, rows, :], e_ref[:, lanes(q)])

    parity = lax.rem(inner, 2)
    own_parity = (parity, 1 - parity)
    top_row = outer == n_outer - 1

    def unit_of(q, late):
        return 2 * q + own_parity[late]

    def copy_to(source, level, u, sem, device):
        return pltpu.make_async_remote_copy(
            src_ref=source,
            dst_ref=got_ref.at[level, u],
            send_sem=sem.at[level, u],
            recv_sem=recv_sem.at[level, u],
            device_id=device,
            device_id_type=MESH,
        )

    def halved(level):
        return inner_bits > 0 and level > inner_bits

    def skips(level, upper):
        return jnp.logical_and(top_row, upper) if level == inner_bits - 1 else None

    def unless(skip, action):
        if skip is None:
            action()
        else:
            pl.when(jnp.logical_not(skip))(action)

    def goes_up(level):
        bit = level - inner_bits
        return jnp.logical_and(outer < n_outer - 1, bit_of(outer + 1, bit) == 1)

    def own_up(level):
        return jnp.logical_and(goes_up(level), bit_of(outer, level - inner_bits) == 0)

    def pass_up(level):
        return jnp.logical_and(goes_up(level), bit_of(outer, level - inner_bits) == 1)

    def inner_copy(level, u):
        return copy_to(agg_ref.at[level, u], level, u, send_sem, {"inner": flipped(level)})

    def up_copy(source, level, u):
        return copy_to(source, level, u, send_sem, {"outer": outer + 1})

    def swap_copy(level, u):
        return copy_to(got_ref.at[level, u], level, u, pass_sem, {"inner": flipped(0)})

    def start_first(q, late):
        if inner_bits:
            u = unit_of(q, 1 - late)
            unless(skips(0, bit_of(inner, 0) == 1), lambda: inner_copy(0, u).start())
        else:
            u = unit_of(q, late)
            pl.when(own_up(0))(lambda: up_copy(agg_ref.at[0, u], 0, u).start())

    def merge(level, u, lower, upper):
        upper_log = upper[N:]
        agg_ref[level + 1, u, 0:N] = jnp.exp(upper_log[0:1]) * lower[0:N] + upper[0:N]
        agg_ref[level + 1, u, N:] = lower[N:] + upper_log

    def handle(level, q, late):
        u = unit_of(q, late)
        got, held = got_ref.at[level, u], agg_ref.at[level, u]
        if level < inner_bits:
            upper = bit_of(inner, level) == 1

            def take():
                inner_copy(level, u).wait_recv()
                following = level + 1
                if following == bits or (late and halved(following)):
                    return

                def join():
                    pl.when(upper)(lambda: merge(level, u, got, held))
                    pl.when(jnp.logical_not(upper))(lambda: merge(level, u, held, got))

                if following < inner_bits:
                    join()
                    unless(
                        skips(following, bit_of(inner, following) == 1),
                        lambda: inner_copy(following, u).start(),
                    )
                    return

                @pl.when(outer < n_outer - 1)
                def _():
                    join()

                @pl.when(own_up(following))
                def _():
                    up_copy(agg_ref.at[following, u], following, u).start()

            unless(skips(level, jnp.logical_not(upper)), take)
            return

        @pl.when(bit_of(outer, level - inner_bits) == 1)
        def _():
            up_copy(held, level, u).wait_recv()
            if late and halved(level):
                return

            @pl.when(pass_up(level))
            def _():
                up_copy(got, level, u).start()

            if halved(level):
                swap_copy(level, u).start()
            following = level + 1
            if following == bits or (late and halved(following)):
                return

            @pl.when(outer < n_outer - 1)
            def _():
                merge(level, u, got, held)

            @pl.when(own_up(following))
            def _():
                up_copy(agg_ref.at[following, u], following, u).start()

    def wait_sent(level, q, late):
        u = unit_of(q, late)
        if level < inner_bits:
            unless(
                skips(level, bit_of(inner, level) == 1),
                lambda: inner_copy(level, u).wait_send(),
            )
            return
        if late and halved(level):
            return
        pl.when(goes_up(level))(lambda: up_copy(agg_ref.at[level, u], level, u).wait_send())
        if halved(level):
            pl.when(bit_of(outer, level - inner_bits) == 1)(
                lambda: swap_copy(level, u).wait_send()
            )

    def needs(level):
        if level < inner_bits:
            return bit_of(inner, level) == 1
        return bit_of(outer, level - inner_bits) == 1

    def near(q):
        state = jnp.zeros((N, LANES), F32)
        total = jnp.zeros((8, LANES), F32)
        for c in range(steps):
            span = slice(c * STEP, (c + 1) * STEP)
            scaled = (v_ref[span, lanes(q)].astype(F32) * weight_of(0, span, q)).astype(BF16)
            log_rows = rows_ref[c, :, lanes(q)]
            factor = jnp.exp(0.5 * log_rows[0:1])
            shrunk = factor * state
            r_ref[c, 0:STEP, lanes(q)] = scaled
            r_ref[c, STEP:, lanes(q)] = shrunk.astype(BF16)
            state = factor * (shrunk + dot(bt_ref[c], scaled))
            total = total + log_rows
        for side in range(2):
            half = slice(side * UNIT, (side + 1) * UNIT)
            agg_ref[0, 2 * q + side, 0:N] = state[:, half]
            agg_ref[0, 2 * q + side, N:] = total[:, half]
        gap_ref[q] = jnp.zeros((8, LANES), F32)

    def local(q):
        for c in range(steps):
            span = slice(c * STEP, (c + 1) * STEP)
            acc_ref[span, lanes(q)] = dot(x_ref[span, :], r_ref[c, :, lanes(q)]) * weight_of(
                1, span, q
            )

    def far(level, q):
        gap = gap_ref[q]
        arrived = jnp.concatenate([got_ref[level, 2 * q], got_ref[level, 2 * q + 1]], axis=1)
        bucket = arrived[0:N] * jnp.exp(gap[0:1])
        gap_ref[q] = gap + arrived[N:]
        high, low = split_two(bucket)
        right = jnp.concatenate([high, low], axis=0)
        for t in range(tokens // FAR_ROWS):
            span = slice(t * FAR_ROWS, (t + 1) * FAR_ROWS)
            left = x_ref[span, STEP:]
            product = dot(jnp.concatenate([left, left], axis=1), right)
            acc_ref[span, lanes(q)] += product * weight_of(2 + level, span, q)

    averaging = (
        lax.broadcasted_iota(jnp.int32, (LANES, LANES), 0) // P_SIZE
        == lax.broadcasted_iota(jnp.int32, (LANES, LANES), 1) // P_SIZE
    )
    averaging = jnp.where(averaging, 1.0 / P_SIZE, 0.0).astype(BF16)

    def finish(q):
        gain = gain_ref[:, lanes(q)]
        for t in range(tokens // FAR_ROWS):
            span = slice(t * FAR_ROWS, (t + 1) * FAR_ROWS)
            combined = acc_ref[span, lanes(q)]
            mean_square = dot((combined * combined).astype(BF16), averaging)
            o_ref[span, lanes(q)] = (
                combined * lax.rsqrt(mean_square + 1e-05) * gain
            ).astype(BF16)

    def out_copy(q):
        span = pl.ds(q * LANES, LANES)
        return pltpu.make_async_copy(o_ref.at[:, span], o_hbm.at[:, span], out_sem.at[q])

    for q in range(chunks):
        v_copies[q].wait()
        near(q)
        if q == 0:
            below = (outer + n_outer - 1) // n_outer
            above = 1 - (outer + 1) // n_outer
            pl.semaphore_wait(barrier, inner_bits + below + above)
        start_first(q, 0)
    for q in range(chunks):
        start_first(q, 1)
    prepare_outputs()
    events = []
    for level in range(bits):
        for late in range(2):
            for q in range(chunks):
                due = q + late * (chunks + 0.5) + 1.6 * level
                events.append((due, level, q, late))
    events.sort()
    for at, (_, level, q, late) in enumerate(events):
        handle(level, q, late)
        if at < chunks:
            local(at)
        if late:
            pl.when(needs(level))(lambda: far(level, q))
            if level == bits - 1:
                finish(q)
                out_copy(q).start()
    for level in range(bits):
        for late in range(2):
            for q in range(chunks):
                wait_sent(level, q, late)
    for q in range(chunks):
        out_copy(q).wait()


def hand_over(source, target, sem):
    copy = pltpu.make_async_copy(source, target, sem)
    copy.start()
    copy.wait()


def per_device(n_outer, n_inner, values, input_state, output_state, decay, gates, gain):
    tokens, width = values.shape
    heads = decay.shape[0]
    bits = n_outer.bit_length() + n_inner.bit_length() - 2
    steps, chunks = tokens // STEP, width // LANES
    units = width // UNIT
    flight = (bits, units, N + 8, UNIT)
    in_hbm = pl.BlockSpec(memory_space=pltpu.HBM)
    anywhere = pl.BlockSpec(memory_space=pl.ANY)
    mixed = pl.pallas_call(
        functools.partial(kernel, n_outer, n_inner),
        out_shape=jax.ShapeDtypeStruct((tokens, width), BF16),
        in_specs=[in_hbm] * 6,
        out_specs=anywhere,
        scratch_shapes=[
            pltpu.VMEM((tokens, width), BF16),
            pltpu.VMEM(input_state.shape, BF16),
            pltpu.VMEM(decay.shape, F32),
            pltpu.VMEM((1, width), F32),
            pltpu.VMEM(output_state.shape, BF16),
            pltpu.VMEM(gates.shape, F32),
            pltpu.VMEM((tokens, width), BF16),
            pltpu.VMEM((2 + bits, tokens, 2 * heads), BF16),
            pltpu.VMEM((2 * heads, width), BF16),
            pltpu.VMEM((steps, N, STEP), BF16),
            pltpu.VMEM((tokens, STEP + N), BF16),
            pltpu.VMEM((steps, STEP + N, width), BF16),
            pltpu.VMEM((steps, 8, width), F32),
            pltpu.VMEM((chunks, 8, LANES), F32),
            pltpu.VMEM((tokens, width), F32),
            pltpu.VMEM(flight, F32),
            pltpu.VMEM(flight, F32),
            pltpu.SemaphoreType.DMA((bits, units)),
            pltpu.SemaphoreType.DMA((bits, units)),
            pltpu.SemaphoreType.DMA((bits, units)),
            pltpu.SemaphoreType.DMA((chunks + 5,)),
            pltpu.SemaphoreType.DMA((chunks,)),
        ],
        compiler_params=pltpu.CompilerParams(
            collective_id=0, has_side_effects=True, vmem_limit_bytes=56 * 1024 * 1024
        ),
    )(values, input_state, output_state, decay, gates, gain.reshape(1, width))
    return pl.pallas_call(
        hand_over,
        out_shape=jax.ShapeDtypeStruct((tokens, width), BF16),
        in_specs=[anywhere],
        out_specs=anywhere,
        scratch_shapes=[pltpu.SemaphoreType.DMA],
        compiler_params=pltpu.CompilerParams(vmem_limit_bytes=1024 * 1024),
    )(mixed)


def solution(mesh):
    sequence = ("outer", "inner")
    return jax.shard_map(
        functools.partial(per_device, mesh.shape["outer"], mesh.shape["inner"]),
        mesh=mesh,
        in_specs=(
            P(sequence, "head"),
            P(sequence, None),
            P(sequence, None),
            P("head", sequence),
            P(None, "head", sequence),
            P("head"),
        ),
        out_specs=P(sequence, "head"),
        check_vma=False,
    )
```
